32 devices in a mesh: gx: 16 (over z, x, core), gy: 2 (over y).
Axes of the slice: x: 2, y: 2, z: 4, core: 2. Of those that a mesh axis runs over, the one named last changes fastest.
Arguments:
- vectors: bfloat16 [64, 16, 128, 128], P('gx', 'gy'), may hold values from -6 to 6
- hamiltonian: bfloat16 [64, 16, 9, 128, 128], P('gx', 'gy'), may hold values from -0.125 to 0.125
- neighbours: int32 [64, 16, 9], P('gx', 'gy'), may hold values from 0 to 8, each once within a row
Outputs:
- filtered: float32 [64, 16, 128, 128], P('gx', 'gy')
The draws below stay inside these ranges and needn't reach their ends.
Inputs may be any that keep to these rules, and one draw needn't show every extreme that they name: `neighbours`: each cell's list names every offset code 0 to 8 exactly once, in any order.
All inputs are finite; a program needn't handle non-finite values.
Results may differ from the reference program's by a relative error of at most 0.0034.
Values may be sent and summed in bfloat16 or wider, within the bound.
A program may use at most 128 MiB of HBM per device.

```python
import jax
import jax.numpy as jnp
from jax import lax

B = 128
M = 128
STEPS = 4
NBR = 9
NCX = 64
NCY = 16


def level_of(key, extent, shards, least, high):
    factor_of, own = 1.0, jax.random.fold_in(key, 6)
    for position, parts in shards:
        heights = jnp.exp(jax.random.uniform(jax.random.fold_in(own, position), (parts,), jnp.float32, least / len(shards), high / len(shards)))
        factor_of = factor_of * jnp.repeat(heights, extent[position] // parts).reshape([-1 if axis == position else 1 for axis in range(len(extent))])
    return factor_of


def noise(stream_key, extent, width, most, cuts=(), kind=jnp.bfloat16):
    drawn = width * jax.random.normal(stream_key, extent, jnp.float32)
    if cuts:
        drawn = drawn * level_of(stream_key, extent, cuts, -0.22, 0.18)
    return jnp.clip(drawn, -most, most).astype(kind)


def setup_inputs(seed: int = 0) -> dict:
    seeds = jax.random.split(jax.random.key(seed), 4)
    return {
        "vectors": noise(seeds[0], (NCX, NCY, B, M), 1.0, 6.0, ((0, 16), (1, 2))),
        "hamiltonian": noise(seeds[1], (NCX, NCY, NBR, B, B), (2 * NBR * B) ** -0.5, 0.125, ((0, 16), (1, 2))),
        "neighbours": jax.vmap(lambda own: jax.random.permutation(own, NBR))(jax.random.split(seeds[2], NCX * NCY)).reshape((NCX, NCY, NBR)).astype(jnp.int32),
    }


def operate(current_b, hamiltonian, neighbours):
    def one_row(row_index):
        nearby = [current_b[(row_index + offset_x) % NCX] for offset_x in (-1, 0, 1)]
        views = []
        for offset_x in (-1, 0, 1):
            for offset_y in (-1, 0, 1):
                views.append(jnp.roll(nearby[offset_x + 1], -offset_y, axis=0))
        stacked = jnp.stack(views, axis=1)
        chosen = jnp.take_along_axis(stacked, neighbours[row_index][:, :, None, None], axis=1)
        return jnp.einsum('ykij,ykjm->yim', hamiltonian[row_index].astype(jnp.float32), chosen.astype(jnp.float32))
    return lax.map(one_row, jnp.arange(NCX, dtype=jnp.int32))


def reference(vectors, hamiltonian, neighbours):
    previous = vectors.astype(jnp.float32)
    current = operate(vectors, hamiltonian, neighbours)
    for step_index in range(1, STEPS):
        following = 2.0 * operate(current.astype(jnp.bfloat16), hamiltonian, neighbours) - previous
        previous = current
        current = following
    return current
```

```python
import functools

import jax
import jax.numpy as jnp
from jax import lax
from jax.experimental import pallas as pl
from jax.experimental.pallas import tpu as pltpu
from jax.sharding import PartitionSpec as P

STEPS = 4
NBR = 9
MESH = pl.DeviceIdType.MESH


def filter_kernel(nx, ny, nb_ref, v_hbm, h_hbm, out_hbm, vbuf, hbuf, ybuf, inv,
                  row_send, row_recv, col_send, col_recv, v_sem, h_sem, out_sem):
    rows, cols = v_hbm.shape[0], v_hbm.shape[1]
    gx, gy = lax.axis_index("gx"), lax.axis_index("gy")
    up = (lax.rem(gx + nx - 1, nx), gy)
    down = (lax.rem(gx + 1, nx), gy)
    left = (gx, lax.rem(gy + ny - 1, ny))
    right = (gx, lax.rem(gy + 1, ny))

    barrier = pltpu.get_barrier_semaphore()
    for neighbour in (up, down, left, right):
        pl.semaphore_signal(barrier, inc=1, device_id=neighbour, device_id_type=MESH)

    v_copy = pltpu.make_async_copy(v_hbm, vbuf.at[0, pl.ds(1, rows), pl.ds(1, cols)], v_sem)
    v_copy.start()
    h_copies = []
    for r in range(rows):
        h_copies.append(pltpu.make_async_copy(h_hbm.at[r], hbuf.at[r], h_sem.at[r]))
        h_copies[-1].start()

    def row_copy(slot, way, c, source=None):
        src_row, dst_row, device = ((1, rows + 1, up), (rows, 0, down))[way]
        src = vbuf.at[slot, src_row, c] if source is None else source
        return pltpu.make_async_remote_copy(
            src_ref=src, dst_ref=vbuf.at[slot, dst_row, c],
            send_sem=row_send.at[slot, way, c], recv_sem=row_recv.at[slot, way, c],
            device_id=device, device_id_type=MESH)

    def col_copy(slot, way, piece, source=None):
        src_col, dst_col, device = ((1, cols + 1, left), (cols, 0, right))[way]
        first, count = ((1, 1), (rows, 1), (2, rows - 2))[piece]
        src = vbuf.at[slot, pl.ds(first, count), src_col]
        if source is not None:
            src = source.at[pl.ds(first - 1, count), src_col - 1]
        return pltpu.make_async_remote_copy(
            src_ref=src, dst_ref=vbuf.at[slot, pl.ds(first, count), dst_col],
            send_sem=col_send.at[slot, way, piece], recv_sem=col_recv.at[slot, way, piece],
            device_id=device, device_id_type=MESH)

    order = []
    for j in range((cols + 1) // 2):
        order.append((j, cols - 1 - j) if j != cols - 1 - j else (j,))

    pl.semaphore_wait(barrier, 4)

    for piece in range(3):
        for way in range(2):
            col_copy(0, way, piece, v_hbm).start()
    for pair in order:
        for j in pair:
            row_copy(0, 0, j + 1, v_hbm.at[0, j]).start()
            row_copy(0, 1, j + 1, v_hbm.at[rows - 1, j]).start()

    def invert(cell, carry):
        r, c = cell // cols, cell % cols
        packed = jnp.int32(0)
        for k in range(NBR):
            code = nb_ref[r, c, k]
            packed = packed + jnp.where(code == NBR - 1, 0, jnp.int32(k) << ((code & 7) * 4))
        total = jnp.int32(0)
        for o in range(NBR - 1):
            entry = jnp.minimum(lax.shift_right_logical(packed, jnp.int32(4 * o)) & 15, NBR - 1)
            inv[cell * NBR + o] = entry
            total = total + entry
        inv[cell * NBR + NBR - 1] = jnp.clip(NBR * (NBR - 1) // 2 - total, 0, NBR - 1)
        return carry

    lax.fori_loop(0, rows * cols, invert, 0)

    v_copy.wait()

    def start_values(r, carry):
        for c in range(cols):
            ybuf[0, r, c] = vbuf[0, r + 1, c + 1].astype(jnp.float32)
            ybuf[1, r, c] = jnp.zeros(ybuf.shape[3:], jnp.float32)
        return carry

    lax.fori_loop(0, rows, start_values, 0)
    for copy in h_copies:
        copy.wait()

    def out_copy(r, c):
        return pltpu.make_async_copy(ybuf.at[0, r, c], out_hbm.at[r, c], out_sem.at[r, c])

    def step(k, last):
        factor = jnp.where(k == 0, 1.0, 2.0).astype(jnp.float32)
        kept = lax.rem(k + 1, 2)

        def cells(places):
            for r, c in places:
                base = (r * cols + c) * NBR
                lhs = jnp.concatenate([hbuf[r, c, inv[base + o]] for o in range(NBR)], axis=1)
                rhs = jnp.concatenate(
                    [vbuf[k, r + o // 3, c + o % 3] for o in range(NBR)], axis=0)
                acc = jnp.dot(lhs, rhs, preferred_element_type=jnp.float32)
                new = factor * acc - ybuf[kept, r, c]
                ybuf[kept, r, c] = new
                if not last:
                    vbuf[k + 1, r + 1, c + 1] = new.astype(jnp.bfloat16)
            if last:
                for r, c in places:
                    out_copy(r, c).start()

        for piece in range(2):
            for way in range(2):
                col_copy(k, way, piece).wait_recv()
        for way in range(2):
            row_copy(k, way, 0).start()
            row_copy(k, way, cols + 1).start()
        for c in range(1, cols - 1):
            cells([(r, c) for r in range(1, rows - 1)])
        for way in range(2):
            col_copy(k, way, 2).wait_recv()
        cells([(r, j) for j in order[0] for r in range(1, rows - 1)])
        if not last:
            for way in range(2):
                col_copy(k + 1, way, 2).start()
        waited = set()
        for number, pair in enumerate(order):
            for j in pair:
                for c in (j, j + 1, j + 2):
                    if c not in waited:
                        waited.add(c)
                        for way in range(2):
                            row_copy(k, way, c).wait_recv()
            cells([(r, j) for j in pair for r in (0, rows - 1)])
            if not last:
                if number == 0:
                    for piece in range(2):
                        for way in range(2):
                            col_copy(k + 1, way, piece).start()
                for j in pair:
                    for way in range(2):
                        row_copy(k + 1, way, j + 1).start()

    def looped(k, carry):
        step(k, False)
        return carry

    lax.fori_loop(0, STEPS - 1, looped, 0)
    step(STEPS - 1, True)

    def drain(k, carry):
        for way in range(2):
            for c in range(cols + 2):
                row_copy(k, way, c).wait_send()
            for piece in range(3):
                col_copy(k, way, piece).wait_send()
        return carry

    lax.fori_loop(0, STEPS, drain, 0)
    for r in range(rows):
        for c in range(cols):
            out_copy(r, c).wait()


def on_device(nx, ny, vectors, hamiltonian, neighbours):
    rows, cols, height, width = vectors.shape
    return pl.pallas_call(
        functools.partial(filter_kernel, nx, ny),
        out_shape=jax.ShapeDtypeStruct(vectors.shape, jnp.float32),
        in_specs=[
            pl.BlockSpec(memory_space=pltpu.SMEM),
            pl.BlockSpec(memory_space=pl.ANY),
            pl.BlockSpec(memory_space=pl.ANY),
        ],
        out_specs=pl.BlockSpec(memory_space=pl.ANY),
        scratch_shapes=[
            pltpu.VMEM((STEPS, rows + 2, cols + 2, height, width), jnp.bfloat16),
            pltpu.VMEM(hamiltonian.shape, jnp.bfloat16),
            pltpu.VMEM((2,) + vectors.shape, jnp.float32),
            pltpu.SMEM((rows * cols * NBR,), jnp.int32),
            pltpu.SemaphoreType.DMA((STEPS, 2, cols + 2)),
            pltpu.SemaphoreType.DMA((STEPS, 2, cols + 2)),
            pltpu.SemaphoreType.DMA((STEPS, 2, 3)),
            pltpu.SemaphoreType.DMA((STEPS, 2, 3)),
            pltpu.SemaphoreType.DMA,
            pltpu.SemaphoreType.DMA((rows,)),
            pltpu.SemaphoreType.DMA((rows, cols)),
        ],
        compiler_params=pltpu.CompilerParams(
            collective_id=0, has_side_effects=True, vmem_limit_bytes=60 * 1024 * 1024),
    )(neighbours, vectors, hamiltonian)


def solution(mesh):
    placed = (P("gx", "gy", None, None), P("gx", "gy", None, None, None), P("gx", "gy", None))
    return jax.shard_map(
        functools.partial(on_device, mesh.shape["gx"], mesh.shape["gy"]),
        mesh=mesh, in_specs=placed, out_specs=P("gx", "gy", None, None), check_vma=False
    )
```

```python
import functools

import jax
import jax.numpy as jnp
from jax import lax
from jax.experimental import pallas as pl
from jax.experimental.pallas import tpu as pltpu
from jax.sharding import PartitionSpec as P

STEPS = 4
NBR = 9
MESH = pl.DeviceIdType.MESH


def filter_kernel(nx, ny, nb_ref, v_hbm, h_hbm, out_hbm, vbuf, hbuf, ybuf, inv,
                  row_send, row_recv, col_send, col_recv, v_sem, h_sem, out_sem):
    rows, cols = v_hbm.shape[0], v_hbm.shape[1]
    gx, gy = lax.axis_index("gx"), lax.axis_index("gy")
    up = (lax.rem(gx + nx - 1, nx), gy)
    down = (lax.rem(gx + 1, nx), gy)
    left = (gx, lax.rem(gy + ny - 1, ny))
    right = (gx, lax.rem(gy + 1, ny))

    parity = lax.rem(gx, 2)
    across = jnp.where(parity == 0, up[0], down[0])
    diagonals = ((across, left[1]), (across, right[1]))

    mirrored = lax.rem(gy, 2) == 1

    def at(p, length):
        return jnp.where(mirrored, length - 1 - p, p)

    near_send = jnp.where(mirrored, 1, 0)
    barrier = pltpu.get_barrier_semaphore()
    for neighbour in (up, down, left, right) + diagonals:
        pl.semaphore_signal(barrier, inc=1, device_id=neighbour, device_id_type=MESH)

    v_copy = pltpu.make_async_copy(v_hbm, vbuf.at[0, pl.ds(1, rows), pl.ds(1, cols)], v_sem)
    v_copy.start()
    h_copies = []
    for r in range(rows):
        h_copies.append(pltpu.make_async_copy(h_hbm.at[r], hbuf.at[r], h_sem.at[r]))
        h_copies[-1].start()

    def row_copy(slot, way, c, source=None):
        src_row, dst_row, device = ((1, rows + 1, up), (rows, 0, down))[way]
        src = vbuf.at[slot, src_row, c] if source is None else source
        return pltpu.make_async_remote_copy(
            src_ref=src, dst_ref=vbuf.at[slot, dst_row, c],
            send_sem=row_send.at[slot, way, c], recv_sem=row_recv.at[slot, way, c],
            device_id=device, device_id_type=MESH)

    def ends(way):
        return (jnp.where(way == 0, 1, cols), jnp.where(way == 0, cols + 1, 0),
                jnp.where(way == 0, left[1], right[1]))

    def diagonal_copy(slot, way, side_way, source=None):
        src_row, dst_row = ((1, rows + 1), (rows, 0))[way]
        src_col, dst_col, place = ends(side_way)
        src = vbuf.at[slot, src_row, src_col]
        if source is not None:
            src = source.at[src_row - 1, src_col - 1]
        return pltpu.make_async_remote_copy(
            src_ref=src, dst_ref=vbuf.at[slot, dst_row, dst_col],
            send_sem=row_send.at[slot, way, dst_col], recv_sem=row_recv.at[slot, way, dst_col],
            device_id=(across, place), device_id_type=MESH)

    def send_corner(slot, side, source=None):
        for way in range(2):
            @pl.when(parity == way)
            def _():
                diagonal_copy(slot, way, send_way(side), source).start()

    def send_way(side):
        return near_send if side == 0 else 1 - near_send

    def col_copy(slot, way, piece, source=None):
        src_col, dst_col, place = ends(way)
        first, count = ((1, 1), (rows, 1), (2, rows - 2))[piece]
        src = vbuf.at[slot, pl.ds(first, count), src_col]
        if source is not None:
            src = source.at[pl.ds(first - 1, count), src_col - 1]
        return pltpu.make_async_remote_copy(
            src_ref=src, dst_ref=vbuf.at[slot, pl.ds(first, count), dst_col],
            send_sem=col_send.at[slot, way, piece], recv_sem=col_recv.at[slot, way, piece],
            device_id=(gx, place), device_id_type=MESH)

    half = (cols + 1) // 2
    halves = (tuple(range(half)), tuple(range(cols - 1, half - 1, -1)))

    pl.semaphore_wait(barrier, 6)

    def pass_corner(slot, side):
        place = at(0 if side == 0 else cols + 1, cols + 2)
        for way in range(2):
            @pl.when(parity != way)
            def _():
                row_copy(slot, way, place).start()

    for side in range(2):
        send_corner(0, side, v_hbm)
        for number, p in enumerate(halves[side]):
            j = at(p, cols)
            row_copy(0, 0, j + 1, v_hbm.at[0, j]).start()
            row_copy(0, 1, j + 1, v_hbm.at[rows - 1, j]).start()
            if number == 0:
                for piece in range(3):
                    col_copy(0, send_way(side), piece, v_hbm).start()

    def invert(cell, carry):
        r, c = cell // cols, cell % cols
        packed = jnp.int32(0)
        for k in range(NBR):
            code = nb_ref[r, c, k]
            packed = packed + jnp.where(code == NBR - 1, 0, jnp.int32(k) << ((code & 7) * 4))
        total = jnp.int32(0)
        for o in range(NBR - 1):
            entry = jnp.minimum(lax.shift_right_logical(packed, jnp.int32(4 * o)) & 15, NBR - 1)
            inv[cell * NBR + o] = entry
            total = total + entry
        inv[cell * NBR + NBR - 1] = jnp.clip(NBR * (NBR - 1) // 2 - total, 0, NBR - 1)
        return carry

    lax.fori_loop(0, rows * cols, invert, 0)

    v_copy.wait()

    def start_values(r, carry):
        for c in range(cols):
            ybuf[0, r, c] = vbuf[0, r + 1, c + 1].astype(jnp.float32)
            ybuf[1, r, c] = jnp.zeros(ybuf.shape[3:], jnp.float32)
        return carry

    lax.fori_loop(0, rows, start_values, 0)
    for copy in h_copies:
        copy.wait()

    def out_copy(r, c):
        return pltpu.make_async_copy(ybuf.at[0, r, c], out_hbm.at[r, c], out_sem.at[r, c])

    def step(k, last):
        factor = jnp.where(k == 0, 1.0, 2.0).astype(jnp.float32)
        kept = lax.rem(k + 1, 2)

        def cells(places):
            for r, c in places:
                base = (r * cols + c) * NBR
                lhs = jnp.concatenate([hbuf[r, c, inv[base + o]] for o in range(NBR)], axis=1)
                rhs = jnp.concatenate(
                    [vbuf[k, r + o // 3, c + o % 3] for o in range(NBR)], axis=0)
                acc = jnp.dot(lhs, rhs, preferred_element_type=jnp.float32)
                new = factor * acc - ybuf[kept, r, c]
                ybuf[kept, r, c] = new
                if not last:
                    vbuf[k + 1, r + 1, c + 1] = new.astype(jnp.bfloat16)
            if last:
                for r, c in places:
                    out_copy(r, c).start()

        waited = set()

        def rim(p, side=None):
            j = at(p, cols)
            for q in (p, p + 1, p + 2):
                if q not in waited:
                    waited.add(q)
                    for way in range(2):
                        row_copy(k, way, at(q, cols + 2)).wait_recv()
            cells([(0, j), (rows - 1, j)])
            if not last:
                if side is not None:
                    send_corner(k + 1, side)
                    for piece in range(2):
                        col_copy(k + 1, send_way(side), piece).start()
                for way in range(2):
                    row_copy(k + 1, way, j + 1).start()

        for side in range(2):
            edge = halves[side][0]
            for piece in range(2):
                col_copy(k, 1 - send_way(side), piece).wait_recv()
            pass_corner(k, side)
            col_copy(k, 1 - send_way(side), 2).wait_recv()
            cells([(r, at(edge, cols)) for r in range(1, rows - 1)])
            if not last:
                col_copy(k + 1, send_way(side), 2).start()
            rim(edge, side)
            for p in halves[side][1:]:
                rim(p)

        for side in range(2):
            for p in halves[side][1:]:
                cells([(r, at(p, cols)) for r in range(1, rows - 1)])

    def looped(k, carry):
        step(k, False)
        return carry

    lax.fori_loop(0, STEPS - 1, looped, 0)
    step(STEPS - 1, True)

    def drain(k, carry):
        for way in range(2):
            for c in range(cols + 2):
                row_copy(k, way, c).wait_send()
            for piece in range(3):
                col_copy(k, way, piece).wait_send()
        return carry

    lax.fori_loop(0, STEPS, drain, 0)
    for r in range(rows):
        for c in range(cols):
            out_copy(r, c).wait()


def on_device(nx, ny, vectors, hamiltonian, neighbours):
    rows, cols, height, width = vectors.shape
    return pl.pallas_call(
        functools.partial(filter_kernel, nx, ny),
        out_shape=jax.ShapeDtypeStruct(vectors.shape, jnp.float32),
        in_specs=[
            pl.BlockSpec(memory_space=pltpu.SMEM),
            pl.BlockSpec(memory_space=pl.ANY),
            pl.BlockSpec(memory_space=pl.ANY),
        ],
        out_specs=pl.BlockSpec(memory_space=pl.ANY),
        scratch_shapes=[
            pltpu.VMEM((STEPS, rows + 2, cols + 2, height, width), jnp.bfloat16),
            pltpu.VMEM(hamiltonian.shape, jnp.bfloat16),
            pltpu.VMEM((2,) + vectors.shape, jnp.float32),
            pltpu.SMEM((rows * cols * NBR,), jnp.int32),
            pltpu.SemaphoreType.DMA((STEPS, 2, cols + 2)),
            pltpu.SemaphoreType.DMA((STEPS, 2, cols + 2)),
            pltpu.SemaphoreType.DMA((STEPS, 2, 3)),
            pltpu.SemaphoreType.DMA((STEPS, 2, 3)),
            pltpu.SemaphoreType.DMA,
            pltpu.SemaphoreType.DMA((rows,)),
            pltpu.SemaphoreType.DMA((rows, cols)),
        ],
        compiler_params=pltpu.CompilerParams(
            collective_id=0, has_side_effects=True, vmem_limit_bytes=60 * 1024 * 1024),
    )(neighbours, vectors, hamiltonian)


def solution(mesh):
    placed = (P("gx", "gy", None, None), P("gx", "gy", None, None, None), P("gx", "gy", None))
    return jax.shard_map(
        functools.partial(on_device, mesh.shape["gx"], mesh.shape["gy"]),
        mesh=mesh, in_specs=placed, out_specs=P("gx", "gy", None, None), check_vma=False
    )
```
